32 devices in a mesh: groups: 2 (over y), seq: 4 (over z), sub: 2 (over x), rep: 2 (over core).
Axes of the slice: x: 2, y: 2, z: 4, core: 2. Of those that a mesh axis runs over, the one named last changes fastest.
Arguments:
- moe_input: bfloat16 [2048, 2048], P(('groups', 'seq'), ('sub', 'rep')), parts along dimension 0, may hold values from -6 to 6
- upstream: bfloat16 [2048, 2048], P(('groups', 'seq'), ('sub', 'rep')), parts along dimension 0, may hold values from -6 to 6
- expert_ids: int32 [2048, 2], P(('groups', 'seq')), parts along dimension 0, may hold values from 0 to 7, all different within a row; in each aligned block of 256 rows (0 to 255, 256 to 511, ...) at most 96 rows name the same one
- router_weight: float32 [2048, 2], P(('groups', 'seq')), parts along dimension 0, may hold values from 0.05 to 1
- w_gate: bfloat16 [8, 2048, 768], P('seq', ('sub', 'rep')), may hold values from -0.125 to 0.125
- w_up: bfloat16 [8, 2048, 768], P('seq', ('sub', 'rep')), may hold values from -0.125 to 0.125
- w_down: bfloat16 [8, 768, 2048], P('seq', None, ('sub', 'rep')), may hold values from -0.21875 to 0.21875
- out_proj: bfloat16 [2048, 2048], P(('sub', 'rep')), may hold values from -0.125 to 0.125
- query: bfloat16 [2048, 2048], P(('groups', 'seq'), ('sub', 'rep')), parts along dimension 0, may hold values from -8 to 8
- key_in: bfloat16 [2048, 2048], P(('groups', 'seq'), ('sub', 'rep')), parts along dimension 0, may hold values from -8 to 8
- value: bfloat16 [2048, 2048], P(('groups', 'seq'), ('sub', 'rep')), parts along dimension 0, may hold values from -6 to 6
Outputs:
- resid_grad: bfloat16 [2048, 2048], P(('groups', 'seq'), ('sub', 'rep')), parts along dimension 0
- query_grad: bfloat16 [2048, 2048], P(('groups', 'seq'), ('sub', 'rep')), parts along dimension 0
- key_grad: bfloat16 [2048, 2048], P(('groups', 'seq'), ('sub', 'rep')), parts along dimension 0
- value_grad: bfloat16 [2048, 2048], P(('groups', 'seq'), ('sub', 'rep')), parts along dimension 0
The draws below stay inside these ranges and needn't reach their ends.
There are 2 independent parts, one for each index of `groups`. The reference program is written for one: setup_inputs(seed, part) draws one part's arguments, and reference() takes and returns one part's arrays. A program takes and returns all parts, laid end to end along the dimension named above; an argument that names none is the same for every part. Nothing has to cross between parts.
Inputs may be any that keep to these rules, and one draw needn't show every extreme that they name: `expert_ids`: each row names two different experts. In each aligned block of 256 rows (the rows of one index of seq) no expert is named by more than 96 rows, a bound that some block reaches.
All inputs are finite; a program needn't handle non-finite values.
Results may differ from the reference program's by a relative error of at most 0.02.
Values may be sent and summed in bfloat16 or wider, within the bound.
No kernel may reach another device: no remote copies, remote signals or barrier semaphores. Data moves between devices by JAX's collectives and lax.ppermute only.
A program may use at most 64 MiB of HBM per device.

```python
import math
import jax
import jax.numpy as jnp
import numpy as np
from jax import lax

D = 2048
FF = 768
HEADS = 16
HEAD_DIM = 128
WINDOW = 128
TOK_SEQ = 256
EXPERTS = 8
TOKENS = 1024
CAP = 96
N_SEQ = 4
N_SUB = 2
N_REP = 2


def paired_rows(key):
    first, second = jax.random.split(jax.random.fold_in(key, 11), 2)
    queries = jax.random.truncated_normal(first, -6.0, 6.0, (TOKENS, D), jnp.float32)
    keys = jax.random.truncated_normal(second, -6.0, 6.0, (TOKENS, D), jnp.float32)
    return (queries, keys)


def draw_query(key, part):
    return paired_rows(key)[0].astype(jnp.bfloat16)


def draw_key_in(key, part):
    return paired_rows(key)[1].astype(jnp.bfloat16)


def shard_levels(own_key, dims, cuts, least, high):
    level = 1.0
    for position, parts in cuts:
        draws = jax.random.uniform(jax.random.fold_in(jax.random.fold_in(own_key, 6), position), (parts,), jnp.float32, least / len(cuts), high / len(cuts))
        level = level * jnp.repeat(jnp.exp(draws), dims[position] // parts).reshape((-1,) + (1,) * (len(dims) - 1 - position))
    return level


def assign_block(own_key, own, number, rows, count, top, bound, lean):
    ranking = jax.random.permutation(own_key, count)
    crowded, usual = portions_of(count, rows * top, bound, lean, True), portions_of(count, rows * top, bound, lean, False)
    places = jnp.arange(count)

    def named(sizes, offset_by):
        used = int((sizes > 0).sum())
        fixed = max(1, used // 4)
        shifted = fixed + (places - fixed + offset_by * (used - fixed)) % max(1, count - fixed)
        return jnp.zeros((count,), jnp.int32).at[ranking[jnp.where(places < fixed, places, shifted)]].set(jnp.asarray(sizes, jnp.int32))

    sizes = jnp.where(number % 4 == 0, named(crowded, number // 4), named(usual, number - number // 4 - 1))
    mixed = jax.random.permutation(jax.random.fold_in(own, 3), count)
    donor, sink = mixed[0:count // 2 * 2:2], mixed[1:count // 2 * 2:2]
    room = jnp.minimum(sizes[donor] - 1, bound - sizes[sink]) // 2
    room = jnp.where((donor == ranking[0]) | (sink == ranking[0]) | (sizes[sink] == 0), 0, jnp.maximum(room, 0))
    shifted = jax.random.randint(jax.random.fold_in(own, 4), (count // 2,), 0, 1 << 20) % (room + 1)
    sizes = sizes.at[donor].add(-shifted).at[sink].add(shifted)
    members = jnp.searchsorted(jnp.cumsum(sizes), jnp.arange(rows * top), side="right").astype(jnp.int32)
    grid = members.reshape(top, rows).T
    grid = grid[jax.random.permutation(jax.random.fold_in(own, 1), rows)]
    offset_by = jax.random.randint(jax.random.fold_in(own, 2), (rows, 1), 0, top)
    return jnp.take_along_axis(grid, (jnp.arange(top)[None, :] + offset_by) % top, axis=1)


def portions_of(number_of, total, bound, skew, full):
    weights = [(1 << 20) // math.isqrt(grade ** skew) + 1 for grade in range(1, number_of + 1)]
    largest = bound if full else min(bound, max(-(-total // number_of), total * weights[0] // sum(weights)))
    least = 1 if total - largest >= number_of - 1 else 0
    counts, surplus = [largest] + [least] * (number_of - 1), total - largest - least * (number_of - 1)
    while surplus > 0:
        free = [i for i in range(1, number_of) if counts[i] < largest] or [i for i in range(1, number_of) if counts[i] < bound]
        mass, remaining = sum([weights[i] for i in free]), surplus
        for i in free:
            more = min(bound - counts[i], max(1, remaining * weights[i] // mass), surplus)
            counts[i] = counts[i] + more
            surplus = surplus - more
    return np.array(counts)


def noise(rng, dims, width, bound, cuts=(), kind=jnp.bfloat16):
    entries = jax.random.normal(rng, dims, jnp.float32) * width
    if len(cuts) > 0:
        entries = shard_levels(rng, dims, cuts, -0.22, 0.18) * entries
    return jnp.clip(entries, min=-bound, max=bound).astype(kind)


def setup_inputs(seed: int = 0, part: int = 0) -> dict:
    seeds = jax.random.split(jax.random.key(seed), 12)
    part_keys = jax.random.split(jax.random.fold_in(seeds[11], part), 12)
    moe_input = noise(part_keys[0], (TOKENS, D), 1.0, 6.0, ((0, 4), (1, 4)))
    upstream = noise(part_keys[1], (TOKENS, D), 1.0, 6.0, ((0, 4), (1, 4)))
    expert_ids_keys = jax.random.split(jax.random.fold_in(part_keys[2], 1), TOKENS // TOK_SEQ)
    expert_ids_turns = jax.random.permutation(jax.random.fold_in(part_keys[2], 3), TOKENS // TOK_SEQ)
    expert_ids = jax.vmap(lambda own, number: assign_block(jax.random.fold_in(part_keys[2], 2), own, number, TOK_SEQ, EXPERTS, 2, CAP, 2))(expert_ids_keys, expert_ids_turns).reshape((TOKENS, 2))
    router_weight = jnp.clip(jnp.exp(math.log(1.0) - 2.9957323 * jax.random.uniform(part_keys[3], (TOKENS, 2), jnp.float32) ** shard_levels(part_keys[3], (TOKENS, 2), ((0, 4),), -0.2, 0.2)), 0.05, 1.0)
    w_gate = noise(seeds[4], (EXPERTS, D, FF), D ** -0.5, 0.125, ((0, 4), (1, 4)))
    w_up = noise(seeds[5], (EXPERTS, D, FF), D ** -0.5, 0.125, ((0, 4), (1, 4)))
    w_down = noise(seeds[6], (EXPERTS, FF, D), FF ** -0.5, 0.21875, ((0, 4), (2, 4)))
    out_proj = noise(seeds[7], (D, D), D ** -0.5, 0.125, ((0, 4),))
    query = draw_query(jax.random.fold_in(jax.random.fold_in(seeds[11], part), 71), part)
    key_in = draw_key_in(jax.random.fold_in(jax.random.fold_in(seeds[11], part), 71), part)
    value = noise(part_keys[10], (TOKENS, D), 1.0, 6.0, ((0, 4), (1, 4)))
    return dict(moe_input=moe_input, upstream=upstream, expert_ids=expert_ids, router_weight=router_weight, w_gate=w_gate, w_up=w_up, w_down=w_down, out_proj=out_proj, query=query, key_in=key_in, value=value)


exact_precision = lax.Precision.HIGHEST

def lower_precision_cast(values_in):
    return lax.optimization_barrier(values_in.astype(jnp.bfloat16)).astype(jnp.float32)

def silu_grads(pre_gate, pre_up, hidden_grad):
    sigmoid_gate = jax.nn.sigmoid(pre_gate)
    gate_grad = hidden_grad * pre_up * sigmoid_gate * (1.0 + pre_gate * (1.0 - sigmoid_gate))
    up_grad = hidden_grad * pre_gate * sigmoid_gate
    return (lower_precision_cast(gate_grad), lower_precision_cast(up_grad))

def expert_grad(operands):
    slot_input, slot_grad, gate_matrix, up_matrix, down_matrix = operands
    pieces = N_SUB * N_REP
    slot_count = slot_input.shape[0]
    width_part = D // pieces
    inputs_split = slot_input.astype(jnp.float32).reshape(slot_count, pieces, width_part)
    grads_split = slot_grad.astype(jnp.float32).reshape(slot_count, pieces, width_part)
    gate_split = gate_matrix.astype(jnp.float32).reshape(pieces, width_part, FF)
    up_split = up_matrix.astype(jnp.float32).reshape(pieces, width_part, FF)
    down_split = down_matrix.astype(jnp.float32).reshape(FF, pieces, width_part)
    pre_gate = lax.optimization_barrier(jnp.sum(lower_precision_cast(jnp.einsum('nfd,fdh->fnh', inputs_split, gate_split, precision=exact_precision)), axis=0))
    pre_up = lax.optimization_barrier(jnp.sum(lower_precision_cast(jnp.einsum('nfd,fdh->fnh', inputs_split, up_split, precision=exact_precision)), axis=0))
    hidden_grad = lax.optimization_barrier(jnp.sum(lower_precision_cast(jnp.einsum('nfd,hfd->fnh', grads_split, down_split, precision=exact_precision)), axis=0))
    gate_grad, up_grad = silu_grads(pre_gate, pre_up, hidden_grad)
    input_grad = jnp.einsum('nh,dh->nd', gate_grad, gate_matrix.astype(jnp.float32), precision=exact_precision)
    input_grad = input_grad + jnp.einsum('nh,dh->nd', up_grad, up_matrix.astype(jnp.float32), precision=exact_precision)
    return input_grad.astype(jnp.bfloat16)

def moe_backward(moe_input, upstream, expert_ids, router_weight, w_gate, w_up, w_down):
    block_pairs = expert_ids.reshape(N_SEQ, 2 * TOK_SEQ)
    one_hot = (block_pairs[:, :, None] == jnp.arange(EXPERTS, dtype=jnp.int32)[None, None, :]).astype(jnp.int32)
    slot_rank = lax.optimization_barrier(jnp.sum((jnp.cumsum(one_hot, axis=1) - one_hot) * one_hot, axis=2))
    block_start = jnp.arange(N_SEQ, dtype=jnp.int32)[:, None] * (EXPERTS * CAP)
    flat_slot = (block_start + block_pairs * CAP + slot_rank).reshape(-1).astype(jnp.int32)
    slot_owner = jnp.zeros((N_SEQ * EXPERTS * CAP,), jnp.int32).at[flat_slot].set(jnp.arange(2 * TOKENS, dtype=jnp.int32) + 1)
    slot_owner = slot_owner.reshape(N_SEQ, EXPERTS, CAP).transpose(1, 0, 2).reshape(EXPERTS, N_SEQ * CAP)
    live_slot = (slot_owner > 0)[:, :, None]
    token_row = jnp.maximum(slot_owner - 1, 0) // 2
    slot_input = jnp.where(live_slot, moe_input[token_row], jnp.zeros((), jnp.bfloat16))
    slot_grad = jnp.where(live_slot, upstream[token_row], jnp.zeros((), jnp.bfloat16))
    slot_out = lax.map(expert_grad, (slot_input, slot_grad, w_gate, w_up, w_down))
    slot_out = slot_out.reshape(EXPERTS, N_SEQ, CAP, D).transpose(1, 0, 2, 3).reshape(N_SEQ * EXPERTS * CAP, D)
    pair_grads = slot_out[flat_slot].astype(jnp.float32) * router_weight.reshape(-1)[:, None]
    combined = upstream.astype(jnp.float32) + lax.optimization_barrier(jnp.sum(pair_grads.reshape(TOKENS, 2, D), axis=1))
    return combined.astype(jnp.bfloat16)

def window_single(queries, keys_ext, values_ext, out_grad, first_key):
    row_count = queries.shape[0]
    key_count = keys_ext.shape[0]
    scaling = HEAD_DIM ** (-0.5)
    query_pos = lax.broadcasted_iota(jnp.int32, (row_count, key_count), 0)
    key_pos = lax.broadcasted_iota(jnp.int32, (row_count, key_count), 1)
    allowed = (key_pos > query_pos) & (key_pos <= query_pos + WINDOW) & (key_pos + first_key >= 0)
    scores = jnp.where(allowed, jnp.dot(queries, keys_ext.T, precision=exact_precision) * scaling, -jnp.inf)
    highest = lax.optimization_barrier(jnp.max(scores, axis=1, keepdims=True))
    weights = jnp.exp(scores - highest)
    softmax_probs = weights / lax.optimization_barrier(jnp.sum(weights, axis=1, keepdims=True))
    probs_low = lower_precision_cast(softmax_probs)
    attended = jnp.dot(probs_low, values_ext, precision=exact_precision)
    centre = lax.optimization_barrier(jnp.sum(out_grad * attended, axis=1))
    prob_grad = jnp.dot(out_grad, values_ext.T, precision=exact_precision)
    score_grad = lower_precision_cast(softmax_probs * (prob_grad - centre[:, None]))
    win_query = jnp.dot(score_grad, keys_ext, precision=exact_precision) * scaling
    win_key = jnp.dot(score_grad.T, queries, precision=exact_precision) * scaling
    win_value = jnp.dot(probs_low.T, out_grad, precision=exact_precision)
    return (win_query, win_key, win_value)

def head_backward(operands):
    queries, keys, values, out_grad = operands
    block_shape = (N_SEQ, TOK_SEQ, HEAD_DIM)
    query_blocks = queries.astype(jnp.float32).reshape(block_shape)
    key_tiles = keys.astype(jnp.float32).reshape(block_shape)
    value_tiles = values.astype(jnp.float32).reshape(block_shape)
    gradient_tiles = out_grad.astype(jnp.float32).reshape(block_shape)
    state_local = jnp.einsum('nsd,nse->nde', key_tiles, value_tiles, precision=exact_precision)
    grad_local = jnp.einsum('nsd,nse->nde', query_blocks, gradient_tiles, precision=exact_precision)
    preceding_state = jnp.cumsum(state_local, axis=0) - state_local
    gradient_following = jnp.cumsum(grad_local[::-1], axis=0)[::-1] - grad_local
    causal_masking = (lax.broadcasted_iota(jnp.int32, (TOK_SEQ, TOK_SEQ), 0) >= lax.broadcasted_iota(jnp.int32, (TOK_SEQ, TOK_SEQ), 1))[None]
    value_products = lower_precision_cast(jnp.where(causal_masking, jnp.einsum('zct,zgt->zcg', gradient_tiles, value_tiles, precision=exact_precision), 0.0))
    query_products = lower_precision_cast(jnp.where(causal_masking, jnp.einsum('nid,njd->nij', query_blocks, key_tiles, precision=exact_precision), 0.0))
    linear_branch_scale = (HEAD_DIM * TOKENS) ** (-0.5)
    linear_query = linear_branch_scale * (jnp.einsum('qxz,qtz->qxt', gradient_tiles, preceding_state, precision=exact_precision) + jnp.einsum('mce,met->mct', value_products, key_tiles, precision=exact_precision))
    lin_key = linear_branch_scale * (jnp.einsum('nje,nde->njd', value_tiles, gradient_following, precision=exact_precision) + jnp.einsum('nij,nid->njd', value_products, query_blocks, precision=exact_precision))
    linear_value = linear_branch_scale * (jnp.einsum('xoq,xqz->xoz', key_tiles, gradient_following, precision=exact_precision) + jnp.einsum('wvg,wvk->wgk', query_products, gradient_tiles, precision=exact_precision))
    halo_zeros = jnp.zeros((1, WINDOW, HEAD_DIM), jnp.float32)
    keys_ext = jnp.concatenate([jnp.concatenate([halo_zeros, key_tiles[:-1, TOK_SEQ - WINDOW:]], axis=0), key_tiles], axis=1)
    values_ext = jnp.concatenate([jnp.concatenate([halo_zeros, value_tiles[:-1, TOK_SEQ - WINDOW:]], axis=0), value_tiles], axis=1)
    first_key = jnp.arange(N_SEQ, dtype=jnp.int32) * TOK_SEQ - WINDOW
    win_query, key_ext_grad, value_ext_grad = jax.vmap(window_single)(query_blocks, keys_ext, values_ext, gradient_tiles, first_key)
    padding = jnp.zeros((N_SEQ, TOK_SEQ - WINDOW, HEAD_DIM), jnp.float32)
    carried_key = jnp.concatenate([key_ext_grad[1:, :WINDOW], halo_zeros], axis=0)
    carried_value = jnp.concatenate([value_ext_grad[1:, :WINDOW], halo_zeros], axis=0)
    win_key = key_ext_grad[:, WINDOW:] + jnp.concatenate([padding, carried_key], axis=1)
    win_value = value_ext_grad[:, WINDOW:] + jnp.concatenate([padding, carried_value], axis=1)
    query_grad = (linear_query + win_query).astype(jnp.bfloat16).reshape(TOKENS, HEAD_DIM)
    key_grad = (lin_key + win_key).astype(jnp.bfloat16).reshape(TOKENS, HEAD_DIM)
    value_grad = (linear_value + win_value).astype(jnp.bfloat16).reshape(TOKENS, HEAD_DIM)
    return (query_grad, key_grad, value_grad)

def by_heads(matrix):
    return matrix.reshape(TOKENS, HEADS, HEAD_DIM).transpose(1, 0, 2)

def from_heads(stacked):
    return stacked.transpose(1, 0, 2).reshape(TOKENS, D)

def reference(moe_input, upstream, expert_ids, router_weight, w_gate, w_up, w_down, out_proj, query, key_in, value):
    resid_grad = moe_backward(moe_input, upstream, expert_ids, router_weight, w_gate, w_up, w_down)
    head_grad = jnp.dot(resid_grad, out_proj.T, preferred_element_type=jnp.float32).astype(jnp.bfloat16)
    query_grad, key_grad, value_grad = lax.map(head_backward, (by_heads(query), by_heads(key_in), by_heads(value), by_heads(head_grad)))
    return (resid_grad, from_heads(query_grad), from_heads(key_grad), from_heads(value_grad))
```

```python
import functools

import jax
import jax.numpy as jnp
from jax import lax
from jax.experimental import pallas as pl
from jax.experimental.pallas import tpu as pltpu
from jax.sharding import PartitionSpec as P

HEAD_DIM = 128
WINDOW = 128
F32 = jnp.float32
BF16 = jnp.bfloat16


def vmem():
    return pl.BlockSpec(memory_space=pltpu.VMEM)


def call(body, outs, args, flops, name):
    moved = sum(a.size * a.dtype.itemsize for a in args) + sum(
        o.size * o.dtype.itemsize for o in outs
    )
    return pl.pallas_call(
        body,
        out_shape=tuple(outs),
        in_specs=[vmem()] * len(args),
        out_specs=tuple([vmem()] * len(outs)),
        cost_estimate=pl.CostEstimate(flops=flops, bytes_accessed=moved, transcendentals=0),
        name=name,
    )(*args)


def shape(dims, dtype=BF16):
    return jax.ShapeDtypeStruct(dims, dtype)


def mm(a, b):
    return lax.dot_general(a, b, (((1,), (0,)), ((), ())), preferred_element_type=F32)


def mm_nt(a, b):
    return lax.dot_general(a, b, (((1,), (1,)), ((), ())), preferred_element_type=F32)


def mm_tn(a, b):
    return lax.dot_general(a, b, (((0,), (0,)), ((), ())), preferred_element_type=F32)


def rotate(value, axis, distance):
    n = lax.axis_size(axis)
    return lax.ppermute(value, axis, [(i, (i + distance) % n) for i in range(n)])


def shift(value, axis, distance):
    n = lax.axis_size(axis)
    return lax.ppermute(
        value, axis, [(i, i + distance) for i in range(n) if 0 <= i + distance < n]
    )


def dispatch_body(n_seq, local, cap, order, ids_ref, x_ref, g_ref, *rest):
    outs, rank_ref = rest[:-1], rest[-1]
    rows = x_ref.shape[0]
    experts = n_seq * local
    first, second = ids_ref[0:1, :], ids_ref[1:2, :]
    expert = lax.broadcasted_iota(jnp.int32, (experts, rows), 0)
    named = (first == expert) | (second == expert)
    earlier = lax.broadcasted_iota(jnp.int32, (rows, rows), 0) < lax.broadcasted_iota(
        jnp.int32, (rows, rows), 1
    )
    rank = mm(named.astype(F32).astype(BF16), earlier.astype(F32).astype(BF16))
    rank_ref[...] = jnp.where(named, rank, -1.0e6)
    me = lax.axis_index("seq")
    slot = lax.broadcasted_iota(jnp.int32, (cap, rows), 0).astype(F32)
    x, g = x_ref[...], g_ref[...]
    for out, delta in zip(outs, order):
        cell = lax.rem(me + delta, n_seq)
        for j in range(local):
            ranks = rank_ref[pl.ds(cell * local + j, 1), :]
            select = (slot == ranks).astype(F32).astype(BF16)
            out[0, j] = mm(select, x).astype(BF16)
            out[1, j] = mm(select, g).astype(BF16)


def dispatch(ids, x, g, n_seq, local, cap, order):
    rows, feats = x.shape
    outs = [shape((2, local, cap, feats)) for _ in order]
    return pl.pallas_call(
        functools.partial(dispatch_body, n_seq, local, cap, order),
        out_shape=tuple(outs),
        in_specs=[vmem()] * 3,
        out_specs=tuple([vmem()] * len(outs)),
        scratch_shapes=[pltpu.VMEM((n_seq * local, rows), F32)],
        cost_estimate=pl.CostEstimate(
            flops=4 * n_seq * local * cap * rows * feats,
            bytes_accessed=8 * rows * feats,
            transcendentals=0,
        ),
        name="dispatch",
    )(ids, x, g)


def partial_body(n_rep, n_sub, count, *refs):
    slots = refs[:count]
    gate, up, down = refs[count : count + 3]
    outs = refs[count + 3 :]
    local, cap = slots[0].shape[1], slots[0].shape[2]
    width = gate.shape[2] // n_rep
    rep = lax.axis_index("rep")
    merge = cap % 16 == 0
    for d in list(range(1, n_rep)) + [0]:
        half = lax.rem(rep + d, n_rep)
        cols = pl.ds(pl.multiple_of(half * width, width), width)
        for j in range(local):
            wg, wu, wd = gate[j, :, cols], up[j, :, cols], down[j, cols, :]
            groups = [list(range(count))] if merge else [[i] for i in range(count)]
            for members in groups:
                x = jnp.concatenate([slots[i][0, j] for i in members], axis=0)
                g = jnp.concatenate([slots[i][1, j] for i in members], axis=0)
                products = (mm(x, wg), mm(x, wu), mm_nt(g, wd))
                for p, product in enumerate(products):
                    for at, i in enumerate(members):
                        unit = j * count + i
                        per = local * count // n_sub
                        outs[d][unit // per, unit % per, p] = product[
                            at * cap : (at + 1) * cap
                        ].astype(BF16)


def partial(slots, gate, up, down, n_rep, n_sub):
    count = len(slots)
    _, local, cap, feats = slots[0].shape
    hidden = gate.shape[2]
    outs = [
        shape((n_sub, local * count // n_sub, 3, cap, hidden // n_rep)) for _ in range(n_rep)
    ]
    return call(
        functools.partial(partial_body, n_rep, n_sub, count),
        outs,
        [*slots, gate, up, down],
        6 * count * local * cap * feats * hidden,
        "partial",
    )


def chip_sum_body(n_sub, count, *refs):
    parts, outs = refs[:count], refs[count:]
    sub = lax.axis_index("sub")
    for d in range(1, n_sub):
        at = lax.rem(sub + d, n_sub)
        total = parts[0][at].astype(F32)
        for part in parts[1:]:
            total = total + part[at].astype(F32)
        outs[d - 1][...] = total.astype(BF16)


def chip_sum(parts, n_sub):
    return call(
        functools.partial(chip_sum_body, n_sub, len(parts)),
        [shape(parts[0].shape[1:]) for _ in range(1, n_sub)],
        parts,
        parts[0].size * len(parts),
        "chip_sum",
    )


def hidden_body(n_own, *refs):
    own, others, out = refs[:n_own], refs[n_own:-1], refs[-1]
    sub = lax.axis_index("sub")
    for u in range(out.shape[0]):
        sums = []
        for p in range(3):
            total = own[0][sub, u, p].astype(F32)
            for part in own[1:]:
                total = total + part[sub, u, p].astype(F32)
            for part in others:
                total = total + part[u, p].astype(F32)
            sums.append(total)
        pre_gate, pre_up, grad = sums
        s = jax.nn.sigmoid(pre_gate)
        out[u, 0] = (grad * pre_up * s * (1.0 + pre_gate * (1.0 - s))).astype(BF16)
        out[u, 1] = (grad * pre_gate * s).astype(BF16)


def hidden(own, others):
    _, units, _, cap, width = own[0].shape
    return call(
        functools.partial(hidden_body, len(own)),
        [shape((units, 2, cap, width))],
        [*own, *others],
        20 * units * cap * width,
        "hidden",
    )[0]


def expert_out_body(n_rep, n_sub, count, *refs):
    pieces = refs[: n_rep * n_sub]
    gate, up = refs[n_rep * n_sub : n_rep * n_sub + 2]
    outs, placed = refs[n_rep * n_sub + 2 : -1], refs[-1]
    local, cap, _ = outs[0].shape
    width = gate.shape[2] // n_rep
    rep, sub = lax.axis_index("rep"), lax.axis_index("sub")
    for dr in range(n_rep):
        for ds in range(n_sub):
            r, q = lax.rem(rep + n_rep - dr, n_rep), lax.rem(sub + n_sub - ds, n_sub)
            placed[r, q] = pieces[dr * n_sub + ds][...]
    per = local * count // n_sub
    merge = cap % 16 == 0
    for j in range(local):
        groups = [list(range(count))] if merge else [[i] for i in range(count)]
        for members in groups:
            total = None
            for r in range(n_rep):
                for p, weight in enumerate((gate, up)):
                    lhs = jnp.concatenate(
                        [
                            placed[r, (j * count + i) // per, (j * count + i) % per, p]
                            for i in members
                        ],
                        axis=0,
                    )
                    term = mm_nt(lhs, weight[j, :, r * width : (r + 1) * width])
                    total = term if total is None else total + term
            for at, i in enumerate(members):
                outs[i][j] = total[at * cap : (at + 1) * cap].astype(BF16)


def expert_out(pieces, gate, up, count, n_rep, n_sub):
    local, feats, hid = gate.shape
    per, _, cap, width = pieces[0].shape
    outs = [shape((local, cap, feats)) for _ in range(count)]
    args = [*pieces, gate, up]
    return pl.pallas_call(
        functools.partial(expert_out_body, n_rep, n_sub, count),
        out_shape=tuple(outs),
        in_specs=[vmem()] * len(args),
        out_specs=tuple([vmem()] * len(outs)),
        scratch_shapes=[pltpu.VMEM((n_rep, n_sub, per, 2, cap, width), BF16)],
        cost_estimate=pl.CostEstimate(
            flops=4 * count * local * cap * feats * hid,
            bytes_accessed=4 * local * feats * hid,
            transcendentals=0,
        ),
        name="expert_out",
    )(*args)


def combine_body(n_seq, order, ids_ref, rw_ref, g_ref, *refs):
    returned, out = refs[:-1], refs[-1]
    rows = g_ref.shape[0]
    local, cap, feats = returned[0].shape
    experts = n_seq * local
    ids = [ids_ref[:, k : k + 1] for k in range(2)]
    expert = lax.broadcasted_iota(jnp.int32, (rows, experts), 1)
    named = (ids[0] == expert) | (ids[1] == expert)
    earlier = lax.broadcasted_iota(jnp.int32, (rows, rows), 0) > lax.broadcasted_iota(
        jnp.int32, (rows, rows), 1
    )
    rank = mm(earlier.astype(F32).astype(BF16), named.astype(F32).astype(BF16))
    me = lax.axis_index("seq")
    slot = lax.broadcasted_iota(jnp.int32, (rows, cap), 1).astype(F32)
    total = g_ref[...].astype(F32)
    for k in range(2):
        at = jnp.sum(jnp.where(ids[k] == expert, rank, 0.0), axis=1, keepdims=True)
        found = None
        for ref, delta in zip(returned, order):
            cell = lax.rem(me + delta, n_seq)
            for j in range(local):
                here = jnp.where(ids[k] == cell * local + j, at, -1.0)
                select = (slot == here).astype(F32).astype(BF16)
                term = mm(select, ref[j])
                found = term if found is None else found + term
        total = total + rw_ref[:, k : k + 1] * found
    out[...] = total.astype(BF16)


def combine(ids, rw, g, returned, n_seq, order):
    rows, feats = g.shape
    return call(
        functools.partial(combine_body, n_seq, order),
        [shape((rows, feats))],
        [ids, rw, g, *returned],
        4 * len(returned) * returned[0].shape[0] * returned[0].shape[1] * rows * feats,
        "combine",
    )[0]


def heads_of(ref, h):
    return ref[:, h * HEAD_DIM : (h + 1) * HEAD_DIM]


def early_body(k_ref, v_ref, state_ref, halo_ref):
    rows = k_ref.shape[0]
    for h in range(state_ref.shape[0]):
        state_ref[h] = mm_tn(heads_of(k_ref, h), heads_of(v_ref, h)).astype(BF16)
    halo_ref[0] = k_ref[rows - WINDOW :, :]
    halo_ref[1] = v_ref[rows - WINDOW :, :]


def project_body(count, w_ref, q_ref, *refs):
    parts, o_ref, state_ref = refs[:count], refs[count], refs[count + 1]
    feats = w_ref.shape[0]
    width = parts[0].shape[1]
    n_rep = lax.axis_size("rep")
    n_sub = lax.axis_size("sub")
    rep, sub = lax.axis_index("rep"), lax.axis_index("sub")
    total = None
    for dr in range(n_rep):
        for ds in range(n_sub):
            r, q = lax.rem(rep + n_rep - dr, n_rep), lax.rem(sub + n_sub - ds, n_sub)
            at = pl.multiple_of((q * n_rep + r) * width, width)
            term = mm_nt(parts[dr * n_sub + ds][...], w_ref[:, pl.ds(at, width)])
            total = term if total is None else total + term
    o_ref[...] = total.astype(BF16)
    for h in range(feats // HEAD_DIM):
        state_ref[h] = mm_tn(heads_of(q_ref, h), heads_of(o_ref, h)).astype(BF16)


def attention_body(
    scale_lin, n_state, q_ref, k_ref, v_ref, o_ref, halo_ref, *refs
):
    states = refs[:n_state]
    dq_ref, dk_ref, dv_ref, carry_ref = refs[n_state:]
    rows = q_ref.shape[0]
    blocks = rows // WINDOW
    scale = HEAD_DIM ** (-0.5)
    first = lax.axis_index("seq") == 0
    r = lax.broadcasted_iota(jnp.int32, (WINDOW, WINDOW), 0)
    c = lax.broadcasted_iota(jnp.int32, (WINDOW, WINDOW), 1)
    lower = r >= c
    upper = r < c
    dk_acc = dk_ref
    for h in range(q_ref.shape[1] // HEAD_DIM):
        cols = slice(h * HEAD_DIM, (h + 1) * HEAD_DIM)

        def block(ref, b):
            return ref[b * WINDOW : (b + 1) * WINDOW, cols]

        before = states[0][h].astype(F32)
        for state in states[1:]:
            before = before + state[h].astype(F32)
        before = (scale_lin * before).astype(BF16)
        q = [block(q_ref, b) for b in range(blocks)]
        o = [block(o_ref, b) for b in range(blocks)]
        k = [block(k_ref, b) for b in range(blocks)]
        v = [block(v_ref, b) for b in range(blocks)]
        k_halo, v_halo = halo_ref[0, :, cols], halo_ref[1, :, cols]
        to_key = {}
        to_value = {}

        def add(table, at, term):
            table[at] = term if at not in table else table[at] + term

        for b in range(blocks):
            k_prev, v_prev = (k[b - 1], v[b - 1]) if b else (k_halo, v_halo)
            qk_own, qk_prev = mm_nt(q[b], k[b]), mm_nt(q[b], k_prev)
            ov_own, ov_prev = mm_nt(o[b], v[b]), mm_nt(o[b], v_prev)
            seen = upper if b else upper & jnp.logical_not(first)
            s_own = jnp.where(lower, qk_own * scale, -jnp.inf)
            s_prev = jnp.where(seen, qk_prev * scale, -jnp.inf)
            top = jnp.maximum(
                jnp.max(s_own, axis=1, keepdims=True), jnp.max(s_prev, axis=1, keepdims=True)
            )
            e_own, e_prev = jnp.exp(s_own - top), jnp.exp(s_prev - top)
            norm = jnp.sum(e_own, axis=1, keepdims=True) + jnp.sum(
                e_prev, axis=1, keepdims=True
            )
            p_own, p_prev = e_own / norm, e_prev / norm
            low_own, low_prev = p_own.astype(BF16), p_prev.astype(BF16)
            attended = mm(low_own, v[b]) + mm(low_prev, v_prev)
            centre = jnp.sum(o[b].astype(F32) * attended, axis=1, keepdims=True)
            g_own = p_own * (ov_own - centre) * scale
            g_prev = p_prev * (ov_prev - centre) * scale
            a_own = (g_own + jnp.where(lower, scale_lin * ov_own, 0.0)).astype(BF16)
            b_own = (p_own + jnp.where(lower, scale_lin * qk_own, 0.0)).astype(BF16)
            if b:
                a_prev = (g_prev + scale_lin * ov_prev).astype(BF16)
                b_prev = (p_prev + scale_lin * qk_prev).astype(BF16)
            else:
                a_prev, b_prev = g_prev.astype(BF16), low_prev
            dq = mm_nt(o[b], before) + mm(a_own, k[b]) + mm(a_prev, k_prev)
            add(to_key, b, mm_tn(a_own, q[b]))
            add(to_key, b - 1, mm_tn(a_prev, q[b]))
            add(to_value, b, mm_tn(b_own, o[b]))
            add(to_value, b - 1, mm_tn(b_prev, o[b]))
            for far in range(b - 1):
                a_far = (scale_lin * mm_nt(o[b], v[far])).astype(BF16)
                b_far = (scale_lin * mm_nt(q[b], k[far])).astype(BF16)
                dq = dq + mm(a_far, k[far])
                add(to_key, far, mm_tn(a_far, q[b]))
                add(to_value, far, mm_tn(b_far, o[b]))
            dq_ref[b * WINDOW : (b + 1) * WINDOW, cols] = dq.astype(BF16)
        for b in range(blocks):
            dk_acc[b * WINDOW : (b + 1) * WINDOW, cols] = to_key[b]
            dv_ref[b * WINDOW : (b + 1) * WINDOW, cols] = to_value[b]
        carry_ref[0, :, cols] = to_key[-1].astype(BF16)
        carry_ref[1, :, cols] = to_value[-1].astype(BF16)


def finish_body(scale_lin, n_state, k_ref, v_ref, dk_ref, dv_ref, carry_ref, *refs):
    states = refs[:n_state]
    ko_ref, vo_ref = refs[n_state:]
    rows = k_ref.shape[0]
    split = rows - WINDOW
    for h in range(k_ref.shape[1] // HEAD_DIM):
        cols = slice(h * HEAD_DIM, (h + 1) * HEAD_DIM)
        after = states[0][h].astype(F32)
        for state in states[1:]:
            after = after + state[h].astype(F32)
        after = (scale_lin * after).astype(BF16)
        dk = dk_ref[:, cols] + mm_nt(v_ref[:, cols], after)
        dv = dv_ref[:, cols] + mm(k_ref[:, cols], after)
        if split:
            ko_ref[:split, cols] = dk[:split].astype(BF16)
            vo_ref[:split, cols] = dv[:split].astype(BF16)
        ko_ref[split:, cols] = (dk[split:] + carry_ref[0, :, cols].astype(F32)).astype(BF16)
        vo_ref[split:, cols] = (dv[split:] + carry_ref[1, :, cols].astype(F32)).astype(BF16)


def plan(n_seq):
    near = [d for i in range(1, n_seq) for d in (i, n_seq - i)]
    order = [0]
    for d in near:
        if d not in order:
            order.append(d)
    parts = min(4, n_seq)
    size = n_seq // parts
    return order, [order[i * size : (i + 1) * size] for i in range(parts)]


def local(
    moe_input,
    upstream,
    expert_ids,
    router_weight,
    w_gate,
    w_up,
    w_down,
    out_proj,
    query,
    key_in,
    value,
):
    rows, feats = moe_input.shape
    n_seq, n_sub, n_rep = (lax.axis_size(a) for a in ("seq", "sub", "rep"))
    local_experts = w_gate.shape[0]
    experts = local_experts * n_seq
    cap = max(2, 3 * rows // experts)
    heads = feats // HEAD_DIM
    scale_lin = (HEAD_DIM * rows * n_seq) ** (-0.5)
    order, chunks = plan(n_seq)

    sends = dict(
        zip(
            order,
            dispatch(expert_ids.T, moe_input, upstream, n_seq, local_experts, cap, order),
        )
    )
    state_local, halo_send = call(
        early_body,
        [shape((heads, HEAD_DIM, HEAD_DIM)), shape((2, WINDOW, feats))],
        [key_in, value],
        2 * rows * feats * HEAD_DIM,
        "early",
    )
    arrived = {0: sends[0]}
    last = None
    for delta in order[1:]:
        send = sends[delta]
        if last is not None and n_seq <= 8:
            send, arrived[last] = lax.optimization_barrier((send, arrived[last]))
        arrived[delta] = rotate(send, "seq", delta)
        last = delta

    returned = {}
    for chunk in chunks:
        count = len(chunk)
        parts = partial([arrived[d] for d in chunk], w_gate, w_up, w_down, n_rep, n_sub)
        own = [parts[0]] + [rotate(parts[d], "rep", d) for d in range(1, n_rep)]
        sums = chip_sum(own, n_sub)
        others = [rotate(sums[d - 1], "sub", d) for d in range(1, n_sub)]
        grads = hidden(own, others)
        across = [grads] + [rotate(grads, "sub", d) for d in range(1, n_sub)]
        pieces = list(across)
        for d in range(1, n_rep):
            pieces += [rotate(piece, "rep", d) for piece in across]
        outs = expert_out(pieces, w_gate, w_up, count, n_rep, n_sub)
        for d, out in zip(chunk, outs):
            returned[d] = rotate(out, "seq", n_seq - d) if d else out

    before = [shift(state_local, "seq", d) for d in range(1, n_seq)]
    halo = shift(halo_send, "seq", 1)

    resid = combine(
        expert_ids, router_weight, upstream, [returned[d] for d in order], n_seq, order
    )
    across = [resid] + [rotate(resid, "sub", d) for d in range(1, n_sub)]
    parts = list(across)
    for d in range(1, n_rep):
        parts += [rotate(part, "rep", d) for part in across]
    head_grad, grad_local = call(
        functools.partial(project_body, len(parts)),
        [shape((rows, feats)), shape((heads, HEAD_DIM, HEAD_DIM))],
        [out_proj, query, *parts],
        2 * rows * out_proj.size,
        "project",
    )
    after = [shift(grad_local, "seq", -d) for d in range(1, n_seq)]
    query_grad, key_part, value_part, carry = call(
        functools.partial(attention_body, scale_lin, len(before)),
        [
            shape((rows, feats)),
            shape((rows, feats), F32),
            shape((rows, feats), F32),
            shape((2, WINDOW, feats)),
        ],
        [query, key_in, value, head_grad, halo, *before],
        60 * heads * WINDOW * WINDOW * HEAD_DIM,
        "attention",
    )
    carried = shift(carry, "seq", -1)
    key_grad, value_grad = call(
        functools.partial(finish_body, scale_lin, len(after)),
        [shape((rows, feats)), shape((rows, feats))],
        [key_in, value, key_part, value_part, carried, *after],
        4 * rows * feats * HEAD_DIM,
        "finish",
    )
    return resid, query_grad, key_grad, value_grad


def solution(mesh):
    rows = P(("groups", "seq"), ("sub", "rep"))
    return jax.shard_map(
        local,
        mesh=mesh,
        in_specs=(
            rows,
            rows,
            P(("groups", "seq"), None),
            P(("groups", "seq"), None),
            P("seq", ("sub", "rep"), None),
            P("seq", ("sub", "rep"), None),
            P("seq", None, ("sub", "rep")),
            P(("sub", "rep"), None),
            rows,
            rows,
            rows,
        ),
        out_specs=(rows, rows, rows, rows),
        check_vma=False,
    )
```
